32 devices in a mesh: replica: 4 (over z), shard: 8 (over y, x, core).
Axes of the slice: x: 2, y: 2, z: 4, core: 2. Of those that a mesh axis runs over, the one named last changes fastest.
Arguments:
- activations: bfloat16 [4, 2048, 4096], P('replica', 'shard'), may hold values from -6 to 6
- head_inputs: bfloat16 [4, 2048, 4096], P('replica', 'shard'), may hold values from -6 to 6
- out_cotangent: bfloat16 [4, 2048, 4096], P('replica', 'shard'), may hold values from -6 to 6
- episode_spans: int32 [4, 4], P('replica'), may hold values from 1 to 8, 16 in all within a row
- last_valid: int32 [4, 4], P('replica'), may hold values from 1 to 128, as said below
- mixer_weight: bfloat16 [4096, 256], P('shard'), may hold values from -0.09375 to 0.09375
- step_weight: bfloat16 [4096, 64], P('shard'), may hold values from -0.09375 to 0.09375
- decay_log: float32 [64], replicated, may hold values from 0 to 2.77
- step_bias: float32 [64], replicated, may hold values from -6.9 to -2.3
- skip_gain: float32 [64], replicated, may hold values from -3 to 3
Outputs:
- inputs_grad: bfloat16 [4, 2048, 4096], P('replica', 'shard')
- activations_grad: bfloat16 [4, 2048, 4096], P('replica', 'shard')
- mixer_grad: float32 [4096, 256], P('shard')
- step_grad: float32 [4096, 64], P('shard')
- decay_grad: float32 [64], replicated
- bias_grad: float32 [64], replicated
- skip_grad: float32 [64], replicated
The draws below stay inside these ranges and needn't reach their ends.
Inputs may be any that keep to these rules, and one draw needn't show every extreme that they name: `episode_spans`: each group's 4 episode lengths, in spans of 128 tokens, add up to 16. `last_valid`: tokens after the valid ones in an episode's last span are padding.
All inputs are finite; a program needn't handle non-finite values.
Results may differ from the reference program's by a relative error of at most 0.018.
Values may be sent and summed in bfloat16 or wider, within the bound.
A program may use at most 320 MiB of HBM per device.

```python
import math
import jax
import jax.numpy as jnp
import numpy as np
from jax import lax

D = 4096
HEADS = 64
STATE = 128
SPAN = 128
EPIS = 4
GROUPS = 4
GROUP_TOK = 2048
GROUP_CH = 16
HP = 4096


def draw_last_valid(key, part):
    total_slots = GROUPS * EPIS
    shortfall = jax.random.randint(jax.random.fold_in(key, 11), (total_slots,), 0, SPAN)
    places = jax.random.permutation(jax.random.fold_in(key, 12), total_slots)
    shortfall = shortfall.at[places[0]].set(0).at[places[1]].set(SPAN - 1)
    return (SPAN - shortfall).reshape(GROUPS, EPIS).astype(jnp.int32)


def strengthened(result, rng, source, target, blocks, factor):
    owner, partner = [(jnp.arange(result.shape[axis_at]) // (result.shape[axis_at] // blocks)).reshape([-1 if axis == axis_at else 1 for axis in range(result.ndim)]) for axis_at in (source, target)]
    chosen = jax.random.permutation(rng, blocks)[partner]
    strong = (owner == chosen) | (owner == (partner + blocks // 2) % blocks)
    return jnp.where(strong, factor * result, result)


def level_of(rng, extent, split, smallest, high):
    gain, own = 1.0, jax.random.fold_in(rng, 6)
    for axis_at, blocks in split:
        draws = jnp.exp(jax.random.uniform(jax.random.fold_in(own, axis_at), (blocks,), jnp.float32, smallest / len(split), high / len(split)))
        gain = gain * jnp.repeat(draws, extent[axis_at] // blocks).reshape([-1 if axis == axis_at else 1 for axis in range(len(extent))])
    return gain


def split_up(count, total, most, lean):
    loads = [(1 << 20) // math.isqrt(rank ** lean) + 1 for rank in range(2, count + 1)]
    surplus, given = total - most - (count - 1), [1] * (count - 1)
    while surplus > 0:
        free = [i for i in range(count - 1) if given[i] < most]
        whole, left = sum([loads[i] for i in free]), surplus
        for i in free:
            extra = min(most - given[i], max(1, left * loads[i] // whole), surplus)
            given[i] = given[i] + extra
            surplus = surplus - extra
    return np.array([most] + given)


def uneven_parts(rng, number_of, total, most, slope):
    if number_of == 2:
        one = jax.random.randint(rng, (), max(1, total - most), min(most, total - 1) + 1)
        return jnp.stack([one, total - one])
    tallies = jnp.asarray(split_up(number_of, total, most, slope), jnp.int32)
    twos = (number_of - 1) // 2
    donor, taker = tallies[1:1 + 2 * twos:2], tallies[2:2 + 2 * twos:2]
    slack = jnp.minimum(donor - 1, most - taker)
    moved = jax.random.randint(jax.random.fold_in(rng, 1), (twos,), 0, 1 << 20) % (slack + 1)
    tallies = tallies.at[1:1 + 2 * twos:2].set(donor - moved).at[2:2 + 2 * twos:2].set(taker + moved)
    return tallies[jax.random.permutation(jax.random.fold_in(rng, 2), number_of)]


def normal_values(key, dims, spread, reach, cuts=(), kind=jnp.bfloat16):
    result = spread * jax.random.normal(key, dims, jnp.float32)
    if cuts:
        result = result * level_of(key, dims, cuts, -0.22, 0.18)
    return jnp.clip(result, -reach, reach).astype(kind)


def bell_draw_with(stream_key, extent, scale, reach, shards, heavy, held_as=jnp.bfloat16):
    values = scale * jax.random.normal(stream_key, extent, jnp.float32)
    if shards:
        values = values * level_of(stream_key, extent, shards, -0.22, 0.18)
    return jnp.clip(strengthened(values, jax.random.fold_in(stream_key, 3), *heavy), -reach, reach).astype(held_as)


def setup_inputs(seed: int = 0) -> dict:
    seeds = jax.random.split(jax.random.key(seed), 11)
    return {
        "activations": bell_draw_with(seeds[0], (GROUPS, GROUP_TOK, D), 1.0, 6.0, ((0, 4), (1, 8)), (1, 2, 8, 2.0)),
        "head_inputs": normal_values(seeds[1], (GROUPS, GROUP_TOK, HP), 1.0, 6.0, ((0, 4), (1, 8))),
        "out_cotangent": normal_values(seeds[2], (GROUPS, GROUP_TOK, HP), 1.0, 6.0, ((0, 4), (1, 8))),
        "episode_spans": jax.vmap(lambda own: uneven_parts(own, EPIS, GROUP_CH, GROUP_CH // 2, 2))(jax.random.split(seeds[3], GROUPS)).reshape((GROUPS, EPIS)).astype(jnp.int32),
        "last_valid": draw_last_valid(jax.random.fold_in(seeds[10], 71), 0),
        "mixer_weight": normal_values(seeds[5], (D, 2 * STATE), D ** -0.5, 0.09375, ((0, 8),)),
        "step_weight": normal_values(seeds[6], (D, HEADS), D ** -0.5, 0.09375, ((0, 8),)),
        "decay_log": jnp.clip(jax.random.uniform(seeds[7], (HEADS,), jnp.float32, 0.0, 2.77), 0.0, 2.77),
        "step_bias": jnp.clip(jax.random.uniform(seeds[8], (HEADS,), jnp.float32, -6.9, -2.3), -6.9, -2.3),
        "skip_gain": normal_values(seeds[9], (HEADS,), 1.0, 3.0, (), jnp.float32),
    }


def span_layout(episode_spans, last_valid, first_span, span_count):
    span_ids = first_span + jnp.arange(span_count, dtype=jnp.int32)
    starts = (jnp.cumsum(episode_spans) - episode_spans).astype(jnp.int32)
    finals = starts + episode_spans - 1
    resets = jnp.any(span_ids[:, None] == starts[None, :], axis=1)
    final_hit = span_ids[:, None] == finals[None, :]
    valid_count = lax.optimization_barrier(jnp.sum(jnp.where(final_hit, last_valid[None, :] - SPAN, 0), axis=1)) + SPAN
    offsets = jnp.arange(SPAN, dtype=jnp.int32)
    valid_mask = jnp.where(offsets[None, :] < valid_count[:, None], 1.0, 0.0).astype(jnp.float32)
    keep_flag = jnp.where(resets, 0.0, 1.0).astype(jnp.float32)
    return (valid_mask, keep_flag)

def span_end(mixers, step_sizes, inputs, decay_log):
    length = inputs.shape[0]
    head_count = decay_log.shape[0]
    per_head = inputs.reshape(length, head_count, -1)
    cumulative = jnp.cumsum(step_sizes * (-jnp.exp(decay_log))[None, :], axis=0)
    weights = jnp.exp(cumulative[-1][None, :] - cumulative) * step_sizes
    weighted = (per_head * weights[:, :, None]).astype(jnp.bfloat16)
    end_state = jnp.einsum('lhp,ln->hpn', weighted.astype(jnp.float32), mixers[:, :STATE].astype(jnp.float32))
    return (jnp.exp(cumulative[-1]), end_state)

def span_out(mixers, step_sizes, inputs, entering, decay_log, skip_gain, valid_mask):
    length = inputs.shape[0]
    head_count = decay_log.shape[0]
    per_head = inputs.reshape(length, head_count, -1)
    input_map = mixers[:, :STATE]
    output_map = mixers[:, STATE:]
    cumulative = jnp.cumsum(step_sizes * (-jnp.exp(decay_log))[None, :], axis=0)
    scores = jnp.dot(output_map, input_map.T, preferred_element_type=jnp.float32)
    by_head = cumulative.T
    causal = jnp.arange(length)[:, None] >= jnp.arange(length)[None, :]
    gaps = jnp.where(causal[None], by_head[:, :, None] - by_head[:, None, :], -jnp.inf)
    mixing = jnp.exp(gaps) * scores[None] * step_sizes.T[:, None, :]
    mixing = mixing.astype(jnp.bfloat16)
    inner = jnp.einsum('hls,shp->lhp', mixing.astype(jnp.float32), per_head.astype(jnp.float32))
    entering_low = entering.astype(jnp.bfloat16)
    carried = jnp.einsum('ln,hpn->lhp', output_map.astype(jnp.float32), entering_low.astype(jnp.float32))
    carried = carried * jnp.exp(cumulative)[:, :, None]
    total = inner + carried + skip_gain[None, :, None] * per_head
    return total.reshape(length, -1) * valid_mask[:, None]

def group_grads(token_rows, head_inputs, out_cotangent, episode_spans, last_valid, mixer_weight, step_weight, decay_log, step_bias, skip_gain):
    valid_mask, keep_flag = span_layout(episode_spans, last_valid, 0, GROUP_CH)
    mixers = jnp.dot(token_rows, mixer_weight, preferred_element_type=jnp.float32).astype(jnp.bfloat16)
    raw_steps = jnp.dot(token_rows, step_weight, preferred_element_type=jnp.float32) + step_bias[None, :]
    flat_mask = valid_mask.reshape(-1)
    out_checked = jax.checkpoint(span_out)

    def scan_model(mixers, raw_steps, head_inputs, decay_log, skip_gain):
        step_sizes = jax.nn.softplus(raw_steps) * flat_mask[:, None]
        mixer_spans = mixers.reshape(GROUP_CH, SPAN, -1)
        step_spans = step_sizes.reshape(GROUP_CH, SPAN, -1)
        input_spans = head_inputs.reshape(GROUP_CH, SPAN, -1)
        decays, states = lax.map(lambda pieces: span_end(pieces[0], pieces[1], pieces[2], decay_log), (mixer_spans, step_spans, input_spans))

        def advance(carry, pieces):
            entering = carry * pieces[2]
            return (pieces[0][:, None, None] * entering + pieces[1], entering)
        start_state = jnp.zeros(states.shape[1:], jnp.float32)
        _, entering = lax.scan(advance, start_state, (decays, states, keep_flag))
        outputs = lax.map(lambda pieces: out_checked(pieces[0], pieces[1], pieces[2], pieces[3], decay_log, skip_gain, pieces[4]), (mixer_spans, step_spans, input_spans, entering, valid_mask))
        return outputs.reshape(GROUP_TOK, -1)
    _, pullback = jax.vjp(scan_model, mixers, raw_steps, head_inputs, decay_log, skip_gain)
    mixer_cot, step_cot, input_grad, decay_grad, skip_grad = pullback(out_cotangent.astype(jnp.float32))
    step_low = step_cot.astype(jnp.bfloat16)
    act_grad = jnp.dot(mixer_cot, mixer_weight.T, preferred_element_type=jnp.float32)
    act_grad = (act_grad + jnp.dot(step_low, step_weight.T, preferred_element_type=jnp.float32)).astype(jnp.bfloat16)
    mixer_wgrad = jnp.dot(token_rows.T, mixer_cot, preferred_element_type=jnp.float32)
    step_wgrad = jnp.dot(token_rows.T, step_low, preferred_element_type=jnp.float32)
    return (input_grad, act_grad, mixer_wgrad, step_wgrad, decay_grad, lax.optimization_barrier(jnp.sum(step_cot, axis=0)), skip_grad)

def reference(activations, head_inputs, out_cotangent, episode_spans, last_valid, mixer_weight, step_weight, decay_log, step_bias, skip_gain):
    results = lax.map(lambda pieces: group_grads(pieces[0], pieces[1], pieces[2], pieces[3], pieces[4], mixer_weight, step_weight, decay_log, step_bias, skip_gain), (activations, head_inputs, out_cotangent, episode_spans, last_valid))
    return (results[0], results[1], lax.optimization_barrier(jnp.sum(results[2], axis=0)), lax.optimization_barrier(jnp.sum(results[3], axis=0)), lax.optimization_barrier(jnp.sum(results[4], axis=0)), lax.optimization_barrier(jnp.sum(results[5], axis=0)), lax.optimization_barrier(jnp.sum(results[6], axis=0)))
```

```python
import jax
import jax.numpy as jnp
from jax import lax
from jax.experimental import pallas as pl
from jax.experimental.pallas import tpu as pltpu
from jax.sharding import PartitionSpec as P

STATE = 128
SPAN = 128
GROUP = 8
F32, BF16 = jnp.float32, jnp.bfloat16


def span_layout(episode_spans, last_valid, first_span, span_count):
    span_ids = first_span + jnp.arange(span_count, dtype=jnp.int32)
    starts = jnp.cumsum(episode_spans) - episode_spans
    finals = starts + episode_spans - 1
    resets = jnp.any(span_ids[:, None] == starts[None, :], axis=1)
    final_hit = span_ids[:, None] == finals[None, :]
    valid_count = jnp.sum(jnp.where(final_hit, last_valid[None, :] - SPAN, 0), axis=1) + SPAN
    offsets = jnp.arange(SPAN, dtype=jnp.int32)
    valid_mask = jnp.where(offsets[None, :] < valid_count[:, None], 1.0, 0.0).astype(jnp.float32)
    keep_flag = jnp.where(resets, 0.0, 1.0).astype(jnp.float32)
    return (valid_mask, keep_flag)


def dot(a, b, ca, cb):
    return lax.dot_general(a, b, (((ca,), (cb,)), ((), ())), preferred_element_type=F32)


def local_kernel(
    x_ref, g_ref, bc_ref, valid_ref, cols_ref, cum_ref, dt_ref, skip_ref,
    dx_ref, end_ref, dent_ref, rowq_ref, colp_ref, ds_ref, skip_out,
):
    group = pl.program_id(1)
    width = x_ref.shape[1] // GROUP
    b, c = bc_ref[:, :STATE], bc_ref[:, STATE:]
    scores = dot(c, b, 1, 1)
    rows = lax.broadcasted_iota(jnp.int32, (SPAN, SPAN), 0)
    lanes = lax.broadcasted_iota(jnp.int32, (SPAN, SPAN), 1)
    causal = rows >= lanes
    lane8 = lax.broadcasted_iota(jnp.int32, (SPAN, GROUP), 1)
    valid = valid_ref[...]
    rowq = jnp.zeros((SPAN, GROUP), F32)
    ds = jnp.zeros((SPAN, SPAN), F32)
    for pair in range(GROUP // 2):
        at = slice(2 * width * pair, 2 * width * (pair + 1))
        first = lanes < width
        x = x_ref[:, at]
        gf = g_ref[:, at].astype(F32) * valid
        xf = x.astype(F32)

        def spread(which):
            two = cols_ref[which, 0, :, 2 * pair : 2 * pair + 2]
            return jnp.where(first, two[:, 0:1], two[:, 1:2])

        skip_out[0, :, at] = jnp.sum(gf * xf, axis=0, keepdims=True)
        dx = gf * skip_ref[:, at]
        for side in range(2):
            h = 2 * pair + side
            mine = first if side == 0 else jnp.logical_not(first)
            gk = jnp.where(mine, gf, 0.0).astype(BF16)
            dm = dot(gk, x, 1, 1).astype(BF16).astype(F32)
            gaps = cols_ref[0, 0, :, h : h + 1] - cum_ref[h : h + 1, :]
            decay = jnp.exp(jnp.where(causal, gaps, -jnp.inf))
            dt = dt_ref[h : h + 1, :]
            plain = decay * scores
            mixing = (plain * dt).astype(BF16)
            dx = dx + dot(mixing, gk, 0, 0)
            part = dm * plain
            colp_ref[h : h + 1, :] = jnp.sum(part, axis=0, keepdims=True)
            rowq = jnp.where(lane8 == h, jnp.sum(part * dt, axis=1, keepdims=True), rowq)
            ds = ds + dm * decay * dt
        dx_ref[:, at] = dx.astype(BF16)
        end_ref[0, at, :] = dot((xf * spread(2)).astype(BF16), b, 0, 0)
        dent_ref[0, at, :] = dot((gf * spread(1)).astype(BF16), c, 0, 0).astype(BF16)
    rowq_ref[0] = rowq

    @pl.when(group == 0)
    def _():
        ds_ref[0] = ds

    @pl.when(group != 0)
    def _():
        ds_ref[0] = ds_ref[0] + ds


def carried_kernel(
    x_ref, g_ref, bc_ref, valid_ref, cols_ref, enter_ref, ends_ref, dx1_ref,
    dx_ref, dcum_ref, dw_ref, dbc_ref, dcot_ref,
):
    group = pl.program_id(1)
    width = x_ref.shape[1] // GROUP
    b, c = bc_ref[:, :STATE], bc_ref[:, STATE:]
    lanes = lax.broadcasted_iota(jnp.int32, (SPAN, SPAN), 1)
    lane8 = lax.broadcasted_iota(jnp.int32, (SPAN, GROUP), 1)
    first = lanes < width
    valid = valid_ref[...]
    dcum = jnp.zeros((SPAN, GROUP), F32)
    dw = jnp.zeros((SPAN, GROUP), F32)
    db = jnp.zeros((SPAN, STATE), F32)
    dc = jnp.zeros((SPAN, STATE), F32)
    for pair in range(GROUP // 2):
        at = slice(2 * width * pair, 2 * width * (pair + 1))
        gf = g_ref[:, at].astype(F32) * valid
        xf = x_ref[:, at].astype(F32)

        def spread(which):
            two = cols_ref[which, 0, :, 2 * pair : 2 * pair + 2]
            return jnp.where(first, two[:, 0:1], two[:, 1:2])

        enter, ends = enter_ref[0, at, :], ends_ref[0, at, :]
        enter_low, ends_low = enter.astype(BF16), ends.astype(BF16)
        w = spread(2)
        ge = gf * spread(1)
        moved = dot(c, enter_low, 1, 1) * ge
        back = dot(b, ends_low, 1, 1).astype(BF16).astype(F32)
        xr = xf * back
        dx_ref[:, at] = (dx1_ref[:, at].astype(F32) + w * back).astype(BF16)
        db = db + dot((xf * w).astype(BF16), ends_low, 1, 0)
        dc = dc + dot(ge.astype(BF16), enter_low, 1, 0)
        prod = enter * ends
        for side in range(2):
            h = 2 * pair + side
            mine = first if side == 0 else jnp.logical_not(first)
            dcum = jnp.where(
                lane8 == h, jnp.sum(jnp.where(mine, moved, 0.0), axis=1, keepdims=True), dcum
            )
            dw = jnp.where(
                lane8 == h, jnp.sum(jnp.where(mine, xr, 0.0), axis=1, keepdims=True), dw
            )
            dcot_ref[0, h : h + 1, :] = jnp.sum(
                prod[side * width : (side + 1) * width], axis=0, keepdims=True
            )
    dcum_ref[0] = dcum
    dw_ref[0] = dw

    @pl.when(group == 0)
    def _():
        dbc_ref[:, :STATE] = db
        dbc_ref[:, STATE:] = dc

    @pl.when(group != 0)
    def _():
        dbc_ref[:, :STATE] = dbc_ref[:, :STATE] + db
        dbc_ref[:, STATE:] = dbc_ref[:, STATE:] + dc


def exchange(forward, backward, factor, width):
    count = lax.axis_size("shard")
    heads = factor.shape[0]
    here = heads // count
    factors = lax.all_gather(factor, "shard")
    both = jnp.stack([forward, backward]).astype(BF16)
    both = both.reshape(2, count, here * width, STATE)
    parts = lax.all_to_all(both, "shard", 1, 1, tiled=True).astype(F32)
    mine = lax.dynamic_slice_in_dim(factors, lax.axis_index("shard") * here, here, 1)
    mine = jnp.repeat(mine, width, axis=1)[:, :, None]
    before, after = [jnp.zeros(parts.shape[2:], F32)], [jnp.zeros(parts.shape[2:], F32)]
    for k in range(count - 1):
        before.append(before[-1] * mine[k] + parts[0, k])
        at = count - 1 - k
        after.append(after[-1] * mine[at] + parts[1, at])
    sent = jnp.stack([jnp.stack(before), jnp.stack(after[::-1])]).astype(BF16)
    got = lax.all_to_all(sent, "shard", 1, 1, tiled=True)
    got = got.reshape(2, heads * width, STATE).astype(F32)
    return got[0], got[1]


def shards(
    activations,
    head_inputs,
    out_cotangent,
    episode_spans,
    last_valid,
    mixer_weight,
    step_weight,
    decay_log,
    step_bias,
    skip_gain,
):
    token_rows = activations[0]
    inputs_here = head_inputs[0]
    cot_here = out_cotangent[0]
    tokens, features = inputs_here.shape
    span_count = tokens // SPAN
    heads = decay_log.shape[0]
    width = features // heads
    groups = heads // GROUP
    block = GROUP * width
    first_span = lax.axis_index("shard") * span_count
    valid_mask, keep_flag = span_layout(episode_spans[0], last_valid[0], first_span, span_count)
    valid = valid_mask.reshape(-1, 1)
    joined = jnp.concatenate([mixer_weight, step_weight], axis=1)
    gathered = lax.all_gather(joined, "shard", axis=0, tiled=True)
    projected = jnp.dot(token_rows, gathered, preferred_element_type=F32)
    mixers = projected[:, : 2 * STATE].astype(BF16)
    raw_steps = projected[:, 2 * STATE :] + step_bias[None, :]
    steps = jax.nn.softplus(raw_steps) * valid
    rate = -jnp.exp(decay_log)
    spans = lambda a: a.reshape(span_count, SPAN, heads)
    cum = jnp.cumsum(spans(steps * rate[None, :]), axis=1)
    last = cum[:, -1]
    tail = jnp.exp(last[:, None] - cum)
    weights = tail * spans(steps)
    decays = jnp.exp(last)
    cols = jnp.stack([cum, jnp.exp(cum), weights]).reshape(3, tokens, groups, GROUP)
    cols = cols.transpose(0, 2, 1, 3)
    cum_rows = cum.reshape(tokens, heads).T
    step_rows = steps.T
    skip_wide = jnp.repeat(skip_gain, width)[None]

    wide = pl.BlockSpec((SPAN, block), lambda s, g: (s, g))
    state = pl.BlockSpec((1, block, STATE), lambda s, g: (s, g, 0))
    mix = pl.BlockSpec((SPAN, 2 * STATE), lambda s, g: (s, 0))
    one = pl.BlockSpec((SPAN, 1), lambda s, g: (s, 0))
    three = pl.BlockSpec((3, 1, SPAN, GROUP), lambda s, g: (0, g, s, 0))
    col = pl.BlockSpec((1, SPAN, GROUP), lambda s, g: (g, s, 0))
    row = pl.BlockSpec((GROUP, SPAN), lambda s, g: (g, s))
    shape = jax.ShapeDtypeStruct
    dx1, ends, dent, rowq, colp, ds, skip_rows = pl.pallas_call(
        local_kernel,
        grid=(span_count, groups),
        in_specs=[wide, wide, mix, one, three, row, row, pl.BlockSpec((1, block), lambda s, g: (0, g))],
        out_specs=[
            wide, state, state, col, row,
            pl.BlockSpec((1, SPAN, SPAN), lambda s, g: (s, 0, 0)),
            pl.BlockSpec((1, 1, block), lambda s, g: (s, 0, g)),
        ],
        out_shape=[
            shape((tokens, features), BF16),
            shape((span_count, features, STATE), F32),
            shape((span_count, features, STATE), BF16),
            shape((groups, tokens, GROUP), F32),
            shape((heads, tokens), F32),
            shape((span_count, SPAN, SPAN), F32),
            shape((span_count, 1, features), F32),
        ],
        name="local",
    )(inputs_here, cot_here, mixers, valid, cols, cum_rows, step_rows, skip_wide)

    factors = decays * keep_flag[:, None]
    factor_wide = jnp.repeat(factors, width, axis=1)[:, :, None]
    dent = dent.astype(F32) * keep_flag[:, None, None]
    total, back_total = ends[0], dent[-1]
    product = factors[0]
    for s in range(1, span_count):
        total = total * factor_wide[s] + ends[s]
        r = span_count - 1 - s
        back_total = back_total * factor_wide[r] + dent[r]
        product = product * factors[s]
    before, after = exchange(total, back_total, product, width)
    entering, ends_grad = [], [None] * span_count
    for s in range(span_count):
        entering.append(before * keep_flag[s])
        before = before * factor_wide[s] + ends[s]
        r = span_count - 1 - s
        ends_grad[r] = after
        after = after * factor_wide[r] + dent[r]
    entering, ends_grad = jnp.stack(entering), jnp.stack(ends_grad)

    input_grad, dcum_out, dw, dbc, dcot = pl.pallas_call(
        carried_kernel,
        grid=(span_count, groups),
        in_specs=[wide, wide, mix, one, three, state, state, wide],
        out_specs=[
            wide, col, col, mix,
            pl.BlockSpec((1, GROUP, STATE), lambda s, g: (s, g, 0)),
        ],
        out_shape=[
            shape((tokens, features), BF16),
            shape((groups, tokens, GROUP), F32),
            shape((groups, tokens, GROUP), F32),
            shape((tokens, 2 * STATE), F32),
            shape((span_count, heads, STATE), F32),
        ],
        name="carried",
    )(inputs_here, cot_here, mixers, valid, cols, entering, ends_grad, dx1)

    flat = lambda a: spans(a.transpose(1, 0, 2).reshape(tokens, heads))
    colp = spans(colp.T)
    dw = flat(dw)
    step_spans = spans(steps)
    dww = dw * weights
    dcum = flat(rowq) - colp * step_spans + flat(dcum_out) - dww
    dlast = jnp.sum(dww, axis=1) + jnp.sum(dcot, axis=-1) * decays
    summed_cum = lax.cumsum(dcum, axis=1, reverse=True) + dlast[:, None]
    dstep = colp + dw * tail + summed_cum * rate
    raw_cot = dstep.reshape(tokens, heads) * valid * jax.nn.sigmoid(raw_steps)
    decay_local = jnp.sum(summed_cum * step_spans, axis=(0, 1)) * rate
    skip_local = jnp.sum(skip_rows.reshape(span_count, heads, width), axis=(0, 2))
    small = lax.psum(
        (decay_local, jnp.sum(raw_cot, axis=0), skip_local), ("replica", "shard")
    )
    mixer_spans = mixers.reshape(span_count, SPAN, 2 * STATE)
    ds_low = ds.astype(BF16)
    db = jnp.einsum("cts,ctn->csn", ds_low, mixer_spans[:, :, STATE:], preferred_element_type=F32)
    dc = jnp.einsum("cts,csn->ctn", ds_low, mixer_spans[:, :, :STATE], preferred_element_type=F32)
    mixer_cot = (dbc + jnp.concatenate([db, dc], axis=2).reshape(tokens, 2 * STATE)).astype(BF16)
    joined_cot = jnp.concatenate([mixer_cot, raw_cot.astype(BF16)], axis=1)
    grads_local = dot(token_rows, joined_cot, 0, 0)
    count = lax.axis_size("shard")
    parts = grads_local.astype(BF16).reshape(count, -1, joined_cot.shape[1])
    parts = lax.all_to_all(parts, "shard", 0, 0, tiled=True)
    shared = jnp.sum(parts.astype(F32), axis=0).astype(BF16)
    summed = jnp.sum(lax.all_gather(shared, "replica").astype(F32), axis=0)
    back_rows = dot(joined_cot, gathered, 1, 1)
    return (
        input_grad[None],
        back_rows.astype(BF16)[None],
        summed[:, : 2 * STATE],
        summed[:, 2 * STATE :],
        small[0],
        small[1],
        small[2],
    )


def solution(mesh):
    return jax.shard_map(
        shards,
        mesh=mesh,
        in_specs=(
            P("replica", "shard", None),
            P("replica", "shard", None),
            P("replica", "shard", None),
            P("replica", None),
            P("replica", None),
            P("shard", None),
            P("shard", None),
            P(),
            P(),
            P(),
        ),
        out_specs=(
            P("replica", "shard", None),
            P("replica", "shard", None),
            P("shard", None),
            P("shard", None),
            P(),
            P(),
            P(),
        ),
        check_vma=False,
    )
```
